32 devices in a mesh: fsdp: 32 (over z, y, x, core).
Axes of the slice: x: 2, y: 2, z: 4, core: 2. Of those that a mesh axis runs over, the one named last changes fastest.
Arguments:
- tokens: bfloat16 [4096, 1024], P('fsdp'), may hold values from -160 to 160
- seq_ids: int32 [4096], P('fsdp'), may hold values from 0 to 64, as said below
- grad_output: bfloat16 [4096, 1024], P('fsdp'), may hold values from -6 to 6
- qkv_weight: bfloat16 [3145728], P('fsdp'), may hold values from -0.1875 to 0.1875
- out_weight: bfloat16 [1048576], P('fsdp'), may hold values from -1 to 1
- up_weight: bfloat16 [4194304], P('fsdp'), may hold values from -0.1875 to 0.1875
- down_weight: bfloat16 [4194304], P('fsdp'), may hold values from -0.09375 to 0.09375
- small_params: bfloat16 [12288], P('fsdp'), may hold values from 0.5 to 1.5
Outputs:
- output: bfloat16 [4096, 1024], P('fsdp')
- tokens_grad: bfloat16 [4096, 1024], P('fsdp')
- qkv_weight_grad: float32 [3145728], P('fsdp')
- out_weight_grad: float32 [1048576], P('fsdp')
- up_weight_grad: float32 [4194304], P('fsdp')
- down_weight_grad: float32 [4194304], P('fsdp')
- small_params_grad: float32 [12288], P('fsdp')
The draws below stay inside these ranges and needn't reach their ends.
Inputs may be any that keep to these rules, and one draw needn't show every extreme that they name: `seq_ids`: within each block of 128 rows the numbers start at 0, rise by one at the first row of each new sequence and never fall; a sequence holds 1 to 64 rows, never crosses a multiple of 64 rows, and every block holds one sequence of exactly 64 rows.
All inputs are finite; a program needn't handle non-finite values.
Results may differ from the reference program's by a relative error of at most 0.012.
The reference program's roundings to bfloat16 on the way count: a program that leaves them out, or rounds other values in their place, can miss the bound.
Values may be sent and summed in bfloat16 or wider, within the bound.
A program may use at most 256 MiB of HBM per device.

```python
import math
import jax
import jax.numpy as jnp
from jax import lax

D = 1024
HEADS = 16
HEAD_DIM = 64
FF = 4096
TOK_DEV = 128
SEQ_MAX = 64
GROUPS = 32
TOKENS = 4096


def draw_tokens(key, part):
    key_base, key_perm = jax.random.split(jax.random.fold_in(key, 11), 2)
    base = jnp.clip(jax.random.normal(key_base, (TOKENS, D), jnp.float32), -4.0, 4.0)
    owner = jax.random.permutation(key_perm, GROUPS)
    column = owner * D // GROUPS
    device_of_row = jnp.arange(TOKENS) // TOK_DEV
    spiked = jnp.arange(D)[None, :] == column[device_of_row][:, None]
    values = jnp.where(spiked, base * 4.0, base)
    return values.astype(jnp.bfloat16)


def draw_seq_ids(key, part):
    key_rate, key_mark, key_long, key_full = jax.random.split(jax.random.fold_in(key, 23), 4)
    levels = jnp.array([48, 12, 3], jnp.int32)
    picked = jax.random.randint(key_rate, (GROUPS, 1), 0, 3)
    threshold = levels[picked]
    marks = jax.random.randint(key_mark, (GROUPS, TOK_DEV), 0, 96) < threshold
    full_group = jax.random.randint(key_full, (), 0, GROUPS)
    marks = marks | (jnp.arange(GROUPS)[:, None] == full_group)
    position = jnp.arange(TOK_DEV)[None, :]
    marks = marks | (position % SEQ_MAX == 0)
    long_block = jax.random.randint(key_long, (GROUPS, 1), 0, TOK_DEV // SEQ_MAX)
    inside_long = (position // SEQ_MAX == long_block) & (position % SEQ_MAX != 0)
    marks = marks & jnp.logical_not(inside_long)
    numbers = jnp.cumsum(marks.astype(jnp.int32), axis=1) - 1
    return numbers.reshape(TOKENS).astype(jnp.int32)


def block_scale(rng, shape, pieces, low, high):
    factor_of, own = 1.0, jax.random.fold_in(rng, 6)
    for dim, parts in pieces:
        steps = jnp.exp(jax.random.uniform(jax.random.fold_in(own, dim), (parts,), jnp.float32, low / len(pieces), high / len(pieces)))
        factor_of = factor_of * jnp.repeat(steps, shape[dim] // parts).reshape([-1 if axis == dim else 1 for axis in range(len(shape))])
    return factor_of


def noise(stream_key, dims, spread, reach, shards=(), held_as=jnp.bfloat16):
    drawn = spread * jax.random.normal(stream_key, dims, jnp.float32)
    if shards:
        drawn = drawn * block_scale(stream_key, dims, shards, -0.22, 0.18)
    return jnp.clip(drawn, -reach, reach).astype(held_as)


def setup_inputs(seed: int = 0) -> dict:
    arg_keys = jax.random.split(jax.random.key(seed), 9)
    tokens = draw_tokens(jax.random.fold_in(arg_keys[8], 71), 0)
    seq_ids = draw_seq_ids(jax.random.fold_in(arg_keys[8], 71), 0)
    grad_output = noise(arg_keys[2], (TOKENS, D), 1.0, 6.0, ((0, 32),))
    qkv_weight = noise(arg_keys[3], (3 * D * D,), D ** -0.5, 0.1875, ((0, 32),))
    out_weight = noise(arg_keys[4], (D * D,), (D // 32) ** -0.5, 1.0, ((0, 32),))
    up_weight = noise(arg_keys[5], (D * FF,), D ** -0.5, 0.1875, ((0, 32),))
    down_weight = noise(arg_keys[6], (FF * D,), FF ** -0.5, 0.09375, ((0, 32),))
    small_params = jnp.clip(1.0 + 0.1 * jax.random.normal(arg_keys[7], (8 * D + FF,), jnp.float32), 0.5, 1.5).astype(jnp.bfloat16)
    return {"tokens": tokens, "seq_ids": seq_ids, "grad_output": grad_output, "qkv_weight": qkv_weight, "out_weight": out_weight, "up_weight": up_weight, "down_weight": down_weight, "small_params": small_params}


EPS = 1e-06
ROOT_HALF = 0.7071067811865476
INV_ROOT_TAU = 0.3989422804014327

def matmul(former, latter):
    return jnp.dot(former, latter, preferred_element_type=jnp.float32)

def matmul_tn(former, latter):
    return jnp.dot(former.T, latter, preferred_element_type=jnp.float32)

def matmul_nt(former, latter):
    return jnp.dot(former, latter.T, preferred_element_type=jnp.float32)

def unpack(params):
    params = params.astype(jnp.float32)
    bounds = [0, D, 2 * D, 3 * D, 4 * D, 5 * D, 5 * D + FF, 6 * D + FF, 7 * D + FF, 8 * D + FF]
    return [params[bounds[position]:bounds[position + 1]] for position in range(9)]

def norm_forward(values, gain, shift):
    center = values - lax.optimization_barrier(jnp.mean(values, axis=-1, keepdims=True))
    inverse = lax.rsqrt(lax.optimization_barrier(jnp.mean(center * center, axis=-1, keepdims=True)) + EPS)
    normed = center * inverse
    return (normed * gain + shift, normed, inverse)

def norm_backward(upstream, normed, inverse, gain):
    scaled = upstream * gain
    return inverse * (scaled - lax.optimization_barrier(jnp.mean(scaled, axis=-1, keepdims=True)) - normed * lax.optimization_barrier(jnp.mean(scaled * normed, axis=-1, keepdims=True)))

def gelu_curve(values):
    return 0.5 * values * (1.0 + lax.erf(values * ROOT_HALF))

def gelu_slope(values):
    return 0.5 * (1.0 + lax.erf(values * ROOT_HALF)) + values * jnp.exp(-0.5 * values * values) * INV_ROOT_TAU

def split_heads(matrix):
    return matrix.reshape(-1, TOK_DEV, HEADS, HEAD_DIM).astype(jnp.float32)

def masked_scores(queries, key_rows, same_seq):
    scores = jnp.einsum('bqhd,bkhd->bhqk', split_heads(queries), split_heads(key_rows)) * HEAD_DIM ** (-0.5)
    return jnp.where(same_seq, scores, -jnp.inf)

def layer_block(inputs, sequence, cotangent, weights):
    qkv_matrix, out_matrix, up_matrix, down_matrix, bias_gain = weights
    query_bias, value_bias, out_bias, gain_one, shift_one, up_bias, down_bias, gain_two, shift_two = unpack(bias_gain)
    seq_blocks = sequence.reshape(-1, TOK_DEV)
    same_seq = (seq_blocks[:, :, None] == seq_blocks[:, None, :])[:, None]
    projected = matmul(inputs, qkv_matrix)
    queries = (projected[:, :D] + query_bias).astype(jnp.bfloat16)
    key_rows = projected[:, D:2 * D].astype(jnp.bfloat16)
    value_rows = (projected[:, 2 * D:] + value_bias).astype(jnp.bfloat16)
    scores = masked_scores(queries, key_rows, same_seq)
    row_max = lax.optimization_barrier(jnp.max(scores, axis=-1, keepdims=True))
    log_total = row_max + jnp.log(lax.optimization_barrier(jnp.sum(jnp.exp(scores - row_max), axis=-1, keepdims=True)))
    attn_probs = jnp.exp(scores - log_total).astype(jnp.bfloat16)
    context = jnp.einsum('bhqk,bkhd->bqhd', attn_probs.astype(jnp.float32), split_heads(value_rows)).reshape(-1, D).astype(jnp.bfloat16)
    first_sum = inputs.astype(jnp.float32) + matmul(context, out_matrix) + out_bias
    first_norm, first_unit, first_inv = norm_forward(first_sum, gain_one, shift_one)
    first_bf = first_norm.astype(jnp.bfloat16)
    hidden_pre = matmul(first_bf, up_matrix) + up_bias
    activated = gelu_curve(hidden_pre).astype(jnp.bfloat16)
    second_sum = first_norm + matmul(activated, down_matrix) + down_bias
    result, second_unit, second_inv = norm_forward(second_sum, gain_two, shift_two)
    out_cot = cotangent.astype(jnp.float32)
    gain_two_grad = lax.optimization_barrier(jnp.sum(out_cot * second_unit, axis=0))
    shift_two_grad = lax.optimization_barrier(jnp.sum(out_cot, axis=0))
    second_grad = norm_backward(out_cot, second_unit, second_inv, gain_two)
    down_bias_grad = lax.optimization_barrier(jnp.sum(second_grad, axis=0))
    second_bf = second_grad.astype(jnp.bfloat16)
    down_grad = matmul_tn(activated, second_bf)
    hidden_grad = matmul_nt(second_bf, down_matrix) * gelu_slope(hidden_pre)
    up_bias_grad = lax.optimization_barrier(jnp.sum(hidden_grad, axis=0))
    hidden_bf = hidden_grad.astype(jnp.bfloat16)
    up_grad = matmul_tn(first_bf, hidden_bf)
    first_grad = second_grad + matmul_nt(hidden_bf, up_matrix)
    gain_one_grad = lax.optimization_barrier(jnp.sum(first_grad * first_unit, axis=0))
    shift_one_grad = lax.optimization_barrier(jnp.sum(first_grad, axis=0))
    residual_grad = norm_backward(first_grad, first_unit, first_inv, gain_one)
    out_bias_grad = lax.optimization_barrier(jnp.sum(residual_grad, axis=0))
    residual_bf = residual_grad.astype(jnp.bfloat16)
    out_grad = matmul_tn(context, residual_bf)
    context_grad = matmul_nt(residual_bf, out_matrix).astype(jnp.bfloat16)
    probs_full = jnp.exp(masked_scores(queries, key_rows, same_seq) - log_total)
    probs_bf = probs_full.astype(jnp.bfloat16)
    prob_grad = jnp.einsum('bqhd,bkhd->bhqk', split_heads(context_grad), split_heads(value_rows))
    value_grad = jnp.einsum('bhqk,bqhd->bkhd', probs_bf.astype(jnp.float32), split_heads(context_grad)).reshape(-1, D)
    row_delta = lax.optimization_barrier(jnp.sum(probs_full * prob_grad, axis=-1, keepdims=True))
    score_grad = (probs_full * (prob_grad - row_delta) * HEAD_DIM ** (-0.5)).astype(jnp.bfloat16)
    query_grad = jnp.einsum('bhqk,bkhd->bqhd', score_grad.astype(jnp.float32), split_heads(key_rows)).reshape(-1, D)
    key_grad = jnp.einsum('bhqk,bqhd->bkhd', score_grad.astype(jnp.float32), split_heads(queries)).reshape(-1, D)
    query_bias_grad = lax.optimization_barrier(jnp.sum(query_grad, axis=0))
    value_bias_grad = lax.optimization_barrier(jnp.sum(value_grad, axis=0))
    joined_bf = jnp.concatenate([query_grad, key_grad, value_grad], axis=1).astype(jnp.bfloat16)
    qkv_grad = matmul_tn(inputs, joined_bf)
    inputs_grad = (residual_grad + matmul_nt(joined_bf, qkv_matrix)).astype(jnp.bfloat16)
    small_grad = jnp.concatenate([query_bias_grad, value_bias_grad, out_bias_grad, gain_one_grad, shift_one_grad, up_bias_grad, down_bias_grad, gain_two_grad, shift_two_grad])
    return (result.astype(jnp.bfloat16), inputs_grad, (qkv_grad, out_grad, up_grad, down_grad, small_grad))

def reference(tokens, seq_ids, grad_output, qkv_weight, out_weight, up_weight, down_weight, small_params):
    weights = (qkv_weight.reshape(D, 3 * D), out_weight.reshape(D, D), up_weight.reshape(D, FF), down_weight.reshape(FF, D), small_params)
    per_step = math.gcd(GROUPS, 32)
    step_count = GROUPS // per_step
    blocks = (tokens.reshape(step_count, per_step * TOK_DEV, D), seq_ids.reshape(step_count, per_step * TOK_DEV), grad_output.reshape(step_count, per_step * TOK_DEV, D))
    zeros = tuple((jnp.zeros(matrix.shape, jnp.float32) for matrix in weights))

    def advance(totals, item):
        result, inputs_grad, grads = layer_block(item[0], item[1], item[2], weights)
        return (tuple((total + grad for total, grad in zip(totals, grads))), (result, inputs_grad))
    totals, (results, input_grads) = lax.scan(advance, zeros, blocks)
    return (results.reshape(TOKENS, D), input_grads.reshape(TOKENS, D), totals[0].reshape(-1), totals[1].reshape(-1), totals[2].reshape(-1), totals[3].reshape(-1), totals[4])
```

```python
import functools

import jax
import jax.numpy as jnp
from jax import lax
from jax.experimental import pallas as pl
from jax.experimental.pallas import tpu as pltpu
from jax.sharding import PartitionSpec as P

D = 1024
HEAD_DIM = 64
FF = 4096
TOK_DEV = 128


EPS = 1e-06
ROOT_HALF = 0.7071067811865476
INV_ROOT_TAU = 0.3989422804014327


def matmul(former, latter):
    return jnp.dot(former, latter, preferred_element_type=jnp.float32)


def matmul_tn(former, latter):
    return lax.dot_general(
        former, latter, (((0,), (0,)), ((), ())), preferred_element_type=jnp.float32
    )


def matmul_nt(former, latter):
    return lax.dot_general(
        former, latter, (((1,), (1,)), ((), ())), preferred_element_type=jnp.float32
    )


def unpack(params):
    params = params.astype(jnp.float32)
    bounds = [0, D, 2 * D, 3 * D, 4 * D, 5 * D, 5 * D + FF, 6 * D + FF, 7 * D + FF, 8 * D + FF]
    return [params[bounds[position] : bounds[position + 1]] for position in range(9)]


def norm_forward(values, gain, shift):
    center = values - jnp.mean(values, axis=-1, keepdims=True)
    inverse = lax.rsqrt(jnp.mean(center * center, axis=-1, keepdims=True) + EPS)
    normed = center * inverse
    return (normed * gain + shift, normed, inverse)


def norm_backward(upstream, normed, inverse, gain):
    scaled = upstream * gain
    return inverse * (
        scaled
        - jnp.mean(scaled, axis=-1, keepdims=True)
        - normed * jnp.mean(scaled * normed, axis=-1, keepdims=True)
    )


def gelu_curve(values):
    return 0.5 * values * (1.0 + lax.erf(values * ROOT_HALF))


def gelu_slope(values):
    return (
        0.5 * (1.0 + lax.erf(values * ROOT_HALF))
        + values * jnp.exp(-0.5 * values * values) * INV_ROOT_TAU
    )


def split_heads(matrix):
    return matrix.reshape(-1, TOK_DEV, matrix.shape[1] // HEAD_DIM, HEAD_DIM)


def block_mask(ids):
    blocks = ids.reshape(-1, TOK_DEV)
    return (blocks[:, :, None] == blocks[:, None, :])[:, None]


def masked_scores(queries, key_rows, same_seq):
    scores = jnp.einsum(
        "bqhd,bkhd->bhqk",
        split_heads(queries),
        split_heads(key_rows),
        preferred_element_type=jnp.float32,
    ) * HEAD_DIM ** (-0.5)
    return jnp.where(same_seq, scores, -jnp.inf)


def attend(queries, key_rows, value_rows, same_seq):
    scores = masked_scores(queries, key_rows, same_seq)
    row_max = jnp.max(scores, axis=-1, keepdims=True)
    log_total = row_max + jnp.log(jnp.sum(jnp.exp(scores - row_max), axis=-1, keepdims=True))
    attn_probs = jnp.exp(scores - log_total).astype(jnp.bfloat16)
    context = (
        jnp.einsum(
            "bhqk,bkhd->bqhd",
            attn_probs,
            split_heads(value_rows),
            preferred_element_type=jnp.float32,
        )
        .reshape(-1, queries.shape[1])
        .astype(jnp.bfloat16)
    )
    return (context, log_total)


def attend_back(queries, key_rows, value_rows, same_seq, log_total, context_grad):
    columns = queries.shape[1]
    probs_full = jnp.exp(masked_scores(queries, key_rows, same_seq) - log_total)
    probs_bf = probs_full.astype(jnp.bfloat16)
    prob_grad = jnp.einsum(
        "bqhd,bkhd->bhqk",
        split_heads(context_grad),
        split_heads(value_rows),
        preferred_element_type=jnp.float32,
    )
    value_grad = jnp.einsum(
        "bhqk,bqhd->bkhd", probs_bf, split_heads(context_grad), preferred_element_type=jnp.float32
    ).reshape(-1, columns)
    row_delta = jnp.sum(probs_full * prob_grad, axis=-1, keepdims=True)
    score_grad = (probs_full * (prob_grad - row_delta) * HEAD_DIM ** (-0.5)).astype(jnp.bfloat16)
    query_grad = jnp.einsum(
        "bhqk,bkhd->bqhd", score_grad, split_heads(key_rows), preferred_element_type=jnp.float32
    ).reshape(-1, columns)
    key_grad = jnp.einsum(
        "bhqk,bqhd->bkhd", score_grad, split_heads(queries), preferred_element_type=jnp.float32
    ).reshape(-1, columns)
    return (query_grad, key_grad, value_grad)


def forward_pass(tokens, seq_ids, weights):
    qkv_matrix, out_matrix, up_matrix, down_matrix, bias_gain = weights
    (
        query_bias,
        value_bias,
        out_bias,
        gain_one,
        shift_one,
        up_bias,
        down_bias,
        gain_two,
        shift_two,
    ) = unpack(bias_gain)
    same_seq = block_mask(seq_ids)
    projected = matmul(tokens, qkv_matrix)
    queries = (projected[:, :D] + query_bias).astype(jnp.bfloat16)
    key_rows = projected[:, D : 2 * D].astype(jnp.bfloat16)
    value_rows = (projected[:, 2 * D :] + value_bias).astype(jnp.bfloat16)
    context, log_total = attend(queries, key_rows, value_rows, same_seq)
    first_sum = tokens.astype(jnp.float32) + matmul(context, out_matrix) + out_bias
    first_norm, first_unit, first_inv = norm_forward(first_sum, gain_one, shift_one)
    first_bf = first_norm.astype(jnp.bfloat16)
    hidden_pre = matmul(first_bf, up_matrix) + up_bias
    activated = gelu_curve(hidden_pre).astype(jnp.bfloat16)
    second_sum = first_norm + matmul(activated, down_matrix) + down_bias
    result, second_unit, second_inv = norm_forward(second_sum, gain_two, shift_two)
    kept = (
        same_seq,
        queries,
        key_rows,
        value_rows,
        log_total,
        context,
        first_unit,
        first_inv,
        first_bf,
        hidden_pre,
        activated,
        second_unit,
        second_inv,
    )
    return (result.astype(jnp.bfloat16), kept)


def mlp_backward(grad_output, kept, weights):
    qkv_matrix, out_matrix, up_matrix, down_matrix, bias_gain = weights
    gain_two = unpack(bias_gain)[7]
    first_bf, hidden_pre, activated, second_unit, second_inv = (
        kept[8],
        kept[9],
        kept[10],
        kept[11],
        kept[12],
    )
    out_cot = grad_output.astype(jnp.float32)
    gain_two_grad = jnp.sum(out_cot * second_unit, axis=0)
    shift_two_grad = jnp.sum(out_cot, axis=0)
    second_grad = norm_backward(out_cot, second_unit, second_inv, gain_two)
    down_bias_grad = jnp.sum(second_grad, axis=0)
    second_bf = second_grad.astype(jnp.bfloat16)
    down_grad = matmul_tn(activated, second_bf)
    hidden_grad = matmul_nt(second_bf, down_matrix) * gelu_slope(hidden_pre)
    up_bias_grad = jnp.sum(hidden_grad, axis=0)
    hidden_bf = hidden_grad.astype(jnp.bfloat16)
    up_grad = matmul_tn(first_bf, hidden_bf)
    first_grad = second_grad + matmul_nt(hidden_bf, up_matrix)
    return (
        first_grad,
        up_grad,
        down_grad,
        (up_bias_grad, down_bias_grad, gain_two_grad, shift_two_grad),
    )


def attention_backward(tokens, first_grad, kept, weights):
    qkv_matrix, out_matrix, up_matrix, down_matrix, bias_gain = weights
    gain_one = unpack(bias_gain)[3]
    same_seq, queries, key_rows, value_rows, log_total, context, first_unit, first_inv = kept[:8]
    gain_one_grad = jnp.sum(first_grad * first_unit, axis=0)
    shift_one_grad = jnp.sum(first_grad, axis=0)
    residual_grad = norm_backward(first_grad, first_unit, first_inv, gain_one)
    out_bias_grad = jnp.sum(residual_grad, axis=0)
    residual_bf = residual_grad.astype(jnp.bfloat16)
    out_grad = matmul_tn(context, residual_bf)
    context_grad = matmul_nt(residual_bf, out_matrix).astype(jnp.bfloat16)
    query_grad, key_grad, value_grad = attend_back(
        queries, key_rows, value_rows, same_seq, log_total, context_grad
    )
    query_bias_grad = jnp.sum(query_grad, axis=0)
    value_bias_grad = jnp.sum(value_grad, axis=0)
    joined_bf = jnp.concatenate([query_grad, key_grad, value_grad], axis=1).astype(jnp.bfloat16)
    qkv_grad = matmul_tn(tokens, joined_bf)
    tokens_grad = (residual_grad + matmul_nt(joined_bf, qkv_matrix)).astype(jnp.bfloat16)
    return (
        tokens_grad,
        qkv_grad,
        out_grad,
        (query_bias_grad, value_bias_grad, out_bias_grad, gain_one_grad, shift_one_grad),
    )


def bit_orders(count):
    bits = count.bit_length() - 1
    first = list(range(bits))
    second = list(first)
    if bits > 2:
        second[1], second[2] = second[2], second[1]
    return first, second


def scatter_sum(partial, order):
    count = lax.axis_size("fsdp")
    me = lax.axis_index("fsdp")
    left = sorted(order, reverse=True)
    held = partial
    for step, bit in enumerate(order):
        place = left.index(bit)
        rows = held.shape[1:]
        split = held.reshape((2**place, 2, 2 ** (len(left) - place - 1)) + rows)
        mine = (me // 2**bit) % 2
        sent = lax.dynamic_index_in_dim(split, 1 - mine, 1, keepdims=False)
        kept = lax.dynamic_index_in_dim(split, mine, 1, keepdims=False)
        got = lax.ppermute(sent, "fsdp", [(i, i ^ (1 << bit)) for i in range(count)])
        total = kept.astype(jnp.float32) + got.astype(jnp.float32)
        left.remove(bit)
        held = total.reshape((2 ** len(left),) + rows)
        if step < len(order) - 1:
            held = held.astype(partial.dtype)
    return held[0]


def row_blocks(matrix):
    count = lax.axis_size("fsdp")
    return matrix.reshape(count, matrix.shape[0] // count, matrix.shape[1])


def gather_kernel(count, plans, arrays, *refs):
    ins, outs = refs[:arrays], refs[arrays : 2 * arrays]
    local_sem, send_sem, recv_sem = refs[2 * arrays :]
    me = lax.axis_index("fsdp")
    bits = count.bit_length() - 1

    def partner(bit):
        return me + 2**bit * (1 - 2 * ((me // 2**bit) % 2))

    barrier = pltpu.get_barrier_semaphore()
    for bit in range(bits):
        pl.semaphore_signal(
            barrier, inc=1, device_id=(partner(bit),), device_id_type=pl.DeviceIdType.MESH
        )
    pl.semaphore_wait(barrier, bits)

    def own_copy(piece):
        array, start, size, _ = plans[piece]
        columns = pl.ds(start, size)
        return pltpu.make_async_copy(
            ins[array].at[:, columns], outs[array].at[me, :, columns], local_sem.at[piece]
        )

    def remote(piece, step, source, target):
        return pltpu.make_async_remote_copy(
            src_ref=source,
            dst_ref=target,
            send_sem=send_sem.at[piece, step],
            recv_sem=recv_sem.at[piece, step],
            device_id=(partner(plans[piece][3][step]),),
            device_id_type=pl.DeviceIdType.MESH,
        )

    def whole(piece, step):
        array, start, size, _ = plans[piece]
        block = outs[array].at[pl.ds(0, 2**step), :, pl.ds(start, size)]
        return remote(piece, step, block, block)

    def begin(piece, step):
        array, start, size, order = plans[piece]
        columns = pl.ds(start, size)
        if step == 0:
            remote(
                piece, step, ins[array].at[:, columns], outs[array].at[me, :, columns]
            ).start()
            return
        base = me
        for bit in order[:step]:
            base = base - ((me // 2**bit) % 2) * 2**bit

        def send(turn, carry):
            row = base
            for position, bit in enumerate(order[:step]):
                row = row + ((turn // 2**position) % 2) * 2**bit
            block = outs[array].at[row, :, columns]
            remote(piece, step, block, block).start()
            return carry

        lax.fori_loop(0, 2**step, send, 0)

    pieces = range(len(plans))
    for piece in pieces:
        begin(piece, 0)
    for piece in pieces:
        own_copy(piece).start()
    for step in range(1, bits):
        for piece in pieces:
            if step == 1:
                own_copy(piece).wait()
            whole(piece, step - 1).wait_recv()
            begin(piece, step)
    for piece in pieces:
        whole(piece, bits - 1).wait_recv()
    for step in range(bits):
        for piece in pieces:
            whole(piece, step).wait_send()


def gather_all(blocks):
    count = lax.axis_size("fsdp")
    first, second = (order[::-1] for order in bit_orders(count))
    wide = [block.shape[1] for block in blocks]
    half = wide[3] // 2
    plans = (
        (0, 0, wide[0], first),
        (1, 0, wide[1], first),
        (2, 0, wide[2], second),
        (3, 0, half, first),
        (3, half, half, second),
        (4, 0, wide[4], second),
    )
    bits = count.bit_length() - 1
    results = pl.pallas_call(
        functools.partial(gather_kernel, count, plans, len(blocks)),
        out_shape=[jax.ShapeDtypeStruct((count,) + block.shape, block.dtype) for block in blocks],
        in_specs=[pl.BlockSpec(memory_space=pltpu.VMEM)] * len(blocks),
        out_specs=[pl.BlockSpec(memory_space=pl.ANY)] * len(blocks),
        scratch_shapes=[
            pltpu.SemaphoreType.DMA((len(plans),)),
            pltpu.SemaphoreType.DMA((len(plans), bits)),
            pltpu.SemaphoreType.DMA((len(plans), bits)),
        ],
        compiler_params=pltpu.CompilerParams(collective_id=0, has_side_effects=True),
    )(*blocks)
    return tuple(result.reshape(-1, result.shape[2]) for result in results[:4]) + (
        results[4].reshape(-1),
    )


def shards(
    tokens, seq_ids, grad_output, qkv_weight, out_weight, up_weight, down_weight, small_params
):
    weights = gather_all(
        (
            qkv_weight.reshape(-1, 3 * D),
            out_weight.reshape(-1, D),
            up_weight.reshape(-1, FF),
            down_weight.reshape(-1, D),
            small_params.reshape(1, -1),
        )
    )
    result, kept = forward_pass(tokens, seq_ids, weights)
    first_grad, up_grad, down_grad, mlp_small = mlp_backward(grad_output, kept, weights)
    first, second = bit_orders(lax.axis_size("fsdp"))
    down_share = scatter_sum(row_blocks(down_grad.astype(jnp.bfloat16)), first)
    up_share = scatter_sum(row_blocks(up_grad.astype(jnp.bfloat16)), second)
    tokens_grad, qkv_grad, out_grad, attn_small = attention_backward(
        tokens, first_grad, kept, weights
    )
    out_share = scatter_sum(row_blocks(out_grad.astype(jnp.bfloat16)), first)
    qkv_blocks = row_blocks(qkv_grad.astype(jnp.bfloat16))
    half = qkv_blocks.shape[2] // 2
    qkv_share = jnp.concatenate(
        [
            scatter_sum(qkv_blocks[:, :, :half], first),
            scatter_sum(qkv_blocks[:, :, half:], second),
        ],
        axis=1,
    )
    small_grad = jnp.concatenate(list(attn_small) + list(mlp_small))
    small_share = scatter_sum(
        small_grad.reshape(lax.axis_size("fsdp"), 1, -1), second
    )
    return (
        result,
        tokens_grad,
        qkv_share.reshape(-1),
        out_share.reshape(-1),
        up_share.reshape(-1),
        down_share.reshape(-1),
        small_share.reshape(-1),
    )


def solution(mesh):
    in_specs = (
        P("fsdp", None),
        P("fsdp"),
        P("fsdp", None),
        P("fsdp"),
        P("fsdp"),
        P("fsdp"),
        P("fsdp"),
        P("fsdp"),
    )
    out_specs = (
        P("fsdp", None),
        P("fsdp", None),
        P("fsdp"),
        P("fsdp"),
        P("fsdp"),
        P("fsdp"),
        P("fsdp"),
    )
    return jax.shard_map(shards, mesh=mesh, in_specs=in_specs, out_specs=out_specs, check_vma=False)
```

```python
import functools

import jax
import jax.numpy as jnp
from jax import lax
from jax.experimental import pallas as pl
from jax.experimental.pallas import tpu as pltpu
from jax.sharding import PartitionSpec as P

D = 1024
HEAD_DIM = 64
FF = 4096
TOK_DEV = 128


EPS = 1e-06
ROOT_HALF = 0.7071067811865476
INV_ROOT_TAU = 0.3989422804014327


def matmul(former, latter):
    return jnp.dot(former, latter, preferred_element_type=jnp.float32)


def matmul_tn(former, latter):
    return lax.dot_general(
        former, latter, (((0,), (0,)), ((), ())), preferred_element_type=jnp.float32
    )


def matmul_nt(former, latter):
    return lax.dot_general(
        former, latter, (((1,), (1,)), ((), ())), preferred_element_type=jnp.float32
    )


def unpack(params):
    params = params.astype(jnp.float32)
    bounds = [0, D, 2 * D, 3 * D, 4 * D, 5 * D, 5 * D + FF, 6 * D + FF, 7 * D + FF, 8 * D + FF]
    return [params[bounds[position] : bounds[position + 1]] for position in range(9)]


def norm_forward(values, gain, shift):
    center = values - jnp.mean(values, axis=-1, keepdims=True)
    inverse = lax.rsqrt(jnp.mean(center * center, axis=-1, keepdims=True) + EPS)
    normed = center * inverse
    return (normed * gain + shift, normed, inverse)


def norm_backward(upstream, normed, inverse, gain):
    scaled = upstream * gain
    return inverse * (
        scaled
        - jnp.mean(scaled, axis=-1, keepdims=True)
        - normed * jnp.mean(scaled * normed, axis=-1, keepdims=True)
    )


def gelu_curve(values):
    return 0.5 * values * (1.0 + lax.erf(values * ROOT_HALF))


def gelu_slope(values):
    return (
        0.5 * (1.0 + lax.erf(values * ROOT_HALF))
        + values * jnp.exp(-0.5 * values * values) * INV_ROOT_TAU
    )


def split_heads(matrix):
    return matrix.reshape(-1, TOK_DEV, matrix.shape[1] // HEAD_DIM, HEAD_DIM)


def block_mask(ids):
    blocks = ids.reshape(-1, TOK_DEV)
    return (blocks[:, :, None] == blocks[:, None, :])[:, None]


def masked_scores(queries, key_rows, same_seq):
    scores = jnp.einsum(
        "bqhd,bkhd->bhqk",
        split_heads(queries),
        split_heads(key_rows),
        preferred_element_type=jnp.float32,
    ) * HEAD_DIM ** (-0.5)
    return jnp.where(same_seq, scores, -jnp.inf)


def attend(queries, key_rows, value_rows, same_seq):
    scores = masked_scores(queries, key_rows, same_seq)
    row_max = jnp.max(scores, axis=-1, keepdims=True)
    log_total = row_max + jnp.log(jnp.sum(jnp.exp(scores - row_max), axis=-1, keepdims=True))
    attn_probs = jnp.exp(scores - log_total).astype(jnp.bfloat16)
    context = (
        jnp.einsum(
            "bhqk,bkhd->bqhd",
            attn_probs,
            split_heads(value_rows),
            preferred_element_type=jnp.float32,
        )
        .reshape(-1, queries.shape[1])
        .astype(jnp.bfloat16)
    )
    return (context, log_total)


def attend_back(queries, key_rows, value_rows, same_seq, log_total, context_grad):
    columns = queries.shape[1]
    probs_full = jnp.exp(masked_scores(queries, key_rows, same_seq) - log_total)
    probs_bf = probs_full.astype(jnp.bfloat16)
    prob_grad = jnp.einsum(
        "bqhd,bkhd->bhqk",
        split_heads(context_grad),
        split_heads(value_rows),
        preferred_element_type=jnp.float32,
    )
    value_grad = jnp.einsum(
        "bhqk,bqhd->bkhd", probs_bf, split_heads(context_grad), preferred_element_type=jnp.float32
    ).reshape(-1, columns)
    row_delta = jnp.sum(probs_full * prob_grad, axis=-1, keepdims=True)
    score_grad = (probs_full * (prob_grad - row_delta) * HEAD_DIM ** (-0.5)).astype(jnp.bfloat16)
    query_grad = jnp.einsum(
        "bhqk,bkhd->bqhd", score_grad, split_heads(key_rows), preferred_element_type=jnp.float32
    ).reshape(-1, columns)
    key_grad = jnp.einsum(
        "bhqk,bqhd->bkhd", score_grad, split_heads(queries), preferred_element_type=jnp.float32
    ).reshape(-1, columns)
    return (query_grad, key_grad, value_grad)


def forward_pass(tokens, seq_ids, weights):
    qkv_matrix, out_matrix, up_matrix, down_matrix, bias_gain = weights
    (
        query_bias,
        value_bias,
        out_bias,
        gain_one,
        shift_one,
        up_bias,
        down_bias,
        gain_two,
        shift_two,
    ) = unpack(bias_gain)
    same_seq = block_mask(seq_ids)
    projected = matmul(tokens, qkv_matrix)
    queries = (projected[:, :D] + query_bias).astype(jnp.bfloat16)
    key_rows = projected[:, D : 2 * D].astype(jnp.bfloat16)
    value_rows = (projected[:, 2 * D :] + value_bias).astype(jnp.bfloat16)
    context, log_total = attend(queries, key_rows, value_rows, same_seq)
    first_sum = tokens.astype(jnp.float32) + matmul(context, out_matrix) + out_bias
    first_norm, first_unit, first_inv = norm_forward(first_sum, gain_one, shift_one)
    first_bf = first_norm.astype(jnp.bfloat16)
    hidden_pre = matmul(first_bf, up_matrix) + up_bias
    activated = gelu_curve(hidden_pre).astype(jnp.bfloat16)
    second_sum = first_norm + matmul(activated, down_matrix) + down_bias
    result, second_unit, second_inv = norm_forward(second_sum, gain_two, shift_two)
    kept = (
        same_seq,
        queries,
        key_rows,
        value_rows,
        log_total,
        context,
        first_unit,
        first_inv,
        first_bf,
        hidden_pre,
        activated,
        second_unit,
        second_inv,
    )
    return (result.astype(jnp.bfloat16), kept)


def mlp_backward(grad_output, kept, weights):
    qkv_matrix, out_matrix, up_matrix, down_matrix, bias_gain = weights
    gain_two = unpack(bias_gain)[7]
    first_bf, hidden_pre, activated, second_unit, second_inv = (
        kept[8],
        kept[9],
        kept[10],
        kept[11],
        kept[12],
    )
    out_cot = grad_output.astype(jnp.float32)
    gain_two_grad = jnp.sum(out_cot * second_unit, axis=0)
    shift_two_grad = jnp.sum(out_cot, axis=0)
    second_grad = norm_backward(out_cot, second_unit, second_inv, gain_two)
    down_bias_grad = jnp.sum(second_grad, axis=0)
    second_bf = second_grad.astype(jnp.bfloat16)
    down_grad = matmul_tn(activated, second_bf)
    hidden_grad = matmul_nt(second_bf, down_matrix) * gelu_slope(hidden_pre)
    up_bias_grad = jnp.sum(hidden_grad, axis=0)
    hidden_bf = hidden_grad.astype(jnp.bfloat16)
    up_grad = matmul_tn(first_bf, hidden_bf)
    first_grad = second_grad + matmul_nt(hidden_bf, up_matrix)
    return (
        first_grad,
        up_grad,
        down_grad,
        (up_bias_grad, down_bias_grad, gain_two_grad, shift_two_grad),
    )


def attention_backward(tokens, first_grad, kept, weights):
    qkv_matrix, out_matrix, up_matrix, down_matrix, bias_gain = weights
    gain_one = unpack(bias_gain)[3]
    same_seq, queries, key_rows, value_rows, log_total, context, first_unit, first_inv = kept[:8]
    gain_one_grad = jnp.sum(first_grad * first_unit, axis=0)
    shift_one_grad = jnp.sum(first_grad, axis=0)
    residual_grad = norm_backward(first_grad, first_unit, first_inv, gain_one)
    out_bias_grad = jnp.sum(residual_grad, axis=0)
    residual_bf = residual_grad.astype(jnp.bfloat16)
    out_grad = matmul_tn(context, residual_bf)
    context_grad = matmul_nt(residual_bf, out_matrix).astype(jnp.bfloat16)
    query_grad, key_grad, value_grad = attend_back(
        queries, key_rows, value_rows, same_seq, log_total, context_grad
    )
    query_bias_grad = jnp.sum(query_grad, axis=0)
    value_bias_grad = jnp.sum(value_grad, axis=0)
    joined_bf = jnp.concatenate([query_grad, key_grad, value_grad], axis=1).astype(jnp.bfloat16)
    qkv_grad = matmul_tn(tokens, joined_bf)
    tokens_grad = (residual_grad + matmul_nt(joined_bf, qkv_matrix)).astype(jnp.bfloat16)
    return (
        tokens_grad,
        qkv_grad,
        out_grad,
        (query_bias_grad, value_bias_grad, out_bias_grad, gain_one_grad, shift_one_grad),
    )


def bit_orders(count):
    bits = count.bit_length() - 1
    first = list(range(bits))
    second, third, fourth = list(first), list(first), list(first)
    if bits > 2:
        second[1], second[2] = 2, 1
    if bits > 3:
        third[1:4] = [3, 1, 2]
        fourth[1:4] = [3, 2, 1]
    return first, second, third, fourth


def column_pieces(widths, parts, orders):
    first, second, third, fourth = orders
    cycle = (first, second, third, first, second, fourth)
    plans = []
    for array, (width, count) in enumerate(zip(widths, parts)):
        size = width // count
        for part in range(count):
            plans.append((array, part * size, size, cycle[len(plans) % len(cycle)]))
    return tuple(plans)


def wavefront(pieces, steps):
    pairs = [(piece, step) for piece in range(pieces) for step in range(steps)]
    return sorted(pairs, key=lambda pair: (pair[0] + 2 * pair[1], -pair[1]))


def row_blocks(matrix):
    count = lax.axis_size("fsdp")
    rows, columns = matrix.shape[0] // count, matrix.shape[1]
    folds = max(1, 16 // rows)
    return matrix.reshape(count, rows * folds, columns // folds)


def scatter_kernel(count, plans, arrays, *refs):
    bits = count.bit_length() - 1
    ins, outs = refs[:arrays], refs[arrays : 2 * arrays]
    held = refs[2 * arrays : 2 * arrays + arrays * bits]
    send_sem, recv_sem = refs[2 * arrays + arrays * bits :]
    me = lax.axis_index("fsdp")

    def side(bit):
        return (me // 2**bit) % 2

    def partner(bit):
        return me + 2**bit * (1 - 2 * side(bit))

    barrier = pltpu.get_barrier_semaphore()
    for bit in range(bits):
        pl.semaphore_signal(
            barrier, inc=1, device_id=(partner(bit),), device_id_type=pl.DeviceIdType.MESH
        )
    pl.semaphore_wait(barrier, bits)

    def remote(piece, step, source, target):
        return pltpu.make_async_remote_copy(
            src_ref=source,
            dst_ref=target,
            send_sem=send_sem.at[piece, step],
            recv_sem=recv_sem.at[piece, step],
            device_id=(partner(plans[piece][3][step]),),
            device_id_type=pl.DeviceIdType.MESH,
        )

    def whole(piece, step):
        array, start, size, _ = plans[piece]
        block = held[array * bits + step].at[:, :, pl.ds(start, size)]
        return remote(piece, step, block, block)

    def spot(piece, step, turn, half):
        order = plans[piece][3]
        if step > 0:
            return 2 * turn + half
        row = half * 2 ** order[0]
        for position, bit in enumerate(order[1:]):
            row = row + ((turn // 2**position) % 2) * 2**bit
        return row

    def source_of(piece, step):
        array = plans[piece][0]
        return ins[array] if step == 0 else held[array * bits + step - 1]

    def begin(piece, step):
        array, start, size, order = plans[piece]
        columns = pl.ds(start, size)
        other = 1 - side(order[step])

        def send(turn, carry):
            remote(
                piece,
                step,
                source_of(piece, step).at[spot(piece, step, turn, other), :, columns],
                held[array * bits + step].at[turn, :, columns],
            ).start()
            return carry

        lax.fori_loop(0, count // 2 ** (step + 1), send, 0)

    def add(piece, step):
        array, start, size, order = plans[piece]
        columns = pl.ds(start, size)
        mine = side(order[step])
        target = held[array * bits + step]

        def one(turn, carry):
            kept = source_of(piece, step)[spot(piece, step, turn, mine), :, columns]
            total = kept.astype(jnp.float32) + target[turn, :, columns].astype(jnp.float32)
            if step == bits - 1:
                outs[array][:, columns] = total
            else:
                target[turn, :, columns] = total.astype(target.dtype)
            return carry

        lax.fori_loop(0, count // 2 ** (step + 1), one, 0)

    for piece in range(len(plans)):
        begin(piece, 0)
    for piece, step in wavefront(len(plans), bits):
        whole(piece, step).wait_recv()
        add(piece, step)
        if step + 1 < bits:
            begin(piece, step + 1)
    for piece in range(len(plans)):
        for step in range(bits):
            whole(piece, step).wait_send()


def scatter_all(blocks):
    count = lax.axis_size("fsdp")
    bits = count.bit_length() - 1
    plans = column_pieces(
        [block.shape[2] for block in blocks], (4, 4, 3, 1, 1), bit_orders(count)
    )
    return pl.pallas_call(
        functools.partial(scatter_kernel, count, plans, len(blocks)),
        out_shape=[jax.ShapeDtypeStruct(block.shape[1:], jnp.float32) for block in blocks],
        in_specs=[pl.BlockSpec(memory_space=pltpu.VMEM)] * len(blocks),
        out_specs=[pl.BlockSpec(memory_space=pltpu.VMEM)] * len(blocks),
        scratch_shapes=[
            pltpu.VMEM((count // 2 ** (step + 1),) + block.shape[1:], block.dtype)
            for block in blocks
            for step in range(bits)
        ]
        + [
            pltpu.SemaphoreType.DMA((len(plans), bits)),
            pltpu.SemaphoreType.DMA((len(plans), bits)),
        ],
        compiler_params=pltpu.CompilerParams(
            collective_id=1, has_side_effects=True, vmem_limit_bytes=64000000
        ),
    )(*blocks)


def gather_kernel(count, plans, arrays, *refs):
    ins, outs = refs[:arrays], refs[arrays : 2 * arrays]
    local_sem, send_sem, recv_sem = refs[2 * arrays :]
    me = lax.axis_index("fsdp")
    bits = count.bit_length() - 1

    def partner(bit):
        return me + 2**bit * (1 - 2 * ((me // 2**bit) % 2))

    barrier = pltpu.get_barrier_semaphore()
    for bit in range(bits):
        pl.semaphore_signal(
            barrier, inc=1, device_id=(partner(bit),), device_id_type=pl.DeviceIdType.MESH
        )
    pl.semaphore_wait(barrier, bits)

    def own_copy(piece):
        array, start, size, _ = plans[piece]
        columns = pl.ds(start, size)
        return pltpu.make_async_copy(
            ins[array].at[:, columns], outs[array].at[me, :, columns], local_sem.at[piece]
        )

    def remote(piece, step, source, target):
        return pltpu.make_async_remote_copy(
            src_ref=source,
            dst_ref=target,
            send_sem=send_sem.at[piece, step],
            recv_sem=recv_sem.at[piece, step],
            device_id=(partner(plans[piece][3][step]),),
            device_id_type=pl.DeviceIdType.MESH,
        )

    def whole(piece, step):
        array, start, size, _ = plans[piece]
        block = outs[array].at[pl.ds(0, 2**step), :, pl.ds(start, size)]
        return remote(piece, step, block, block)

    def begin(piece, step):
        array, start, size, order = plans[piece]
        columns = pl.ds(start, size)
        if step == 0:
            remote(
                piece, step, ins[array].at[:, columns], outs[array].at[me, :, columns]
            ).start()
            return
        base = me
        for bit in order[:step]:
            base = base - ((me // 2**bit) % 2) * 2**bit

        def send(turn, carry):
            row = base
            for position, bit in enumerate(order[:step]):
                row = row + ((turn // 2**position) % 2) * 2**bit
            block = outs[array].at[row, :, columns]
            remote(piece, step, block, block).start()
            return carry

        lax.fori_loop(0, 2**step, send, 0)

    pieces = range(len(plans))
    for piece in pieces:
        begin(piece, 0)
    for piece in pieces:
        own_copy(piece).start()
    for piece, step in wavefront(len(plans), bits):
        whole(piece, step).wait_recv()
        if step == 0:
            own_copy(piece).wait()
        if step + 1 < bits:
            begin(piece, step + 1)
    for step in range(bits):
        for piece in pieces:
            whole(piece, step).wait_send()


def gather_all(blocks):
    count = lax.axis_size("fsdp")
    plans = column_pieces(
        [block.shape[1] for block in blocks],
        (3, 1, 4, 4, 1),
        [order[::-1] for order in bit_orders(count)],
    )
    bits = count.bit_length() - 1
    results = pl.pallas_call(
        functools.partial(gather_kernel, count, plans, len(blocks)),
        out_shape=[jax.ShapeDtypeStruct((count,) + block.shape, block.dtype) for block in blocks],
        in_specs=[pl.BlockSpec(memory_space=pltpu.VMEM)] * len(blocks),
        out_specs=[pl.BlockSpec(memory_space=pl.ANY)] * len(blocks),
        scratch_shapes=[
            pltpu.SemaphoreType.DMA((len(plans),)),
            pltpu.SemaphoreType.DMA((len(plans), bits)),
            pltpu.SemaphoreType.DMA((len(plans), bits)),
        ],
        compiler_params=pltpu.CompilerParams(collective_id=0, has_side_effects=True),
    )(*blocks)
    return tuple(result.reshape(-1, result.shape[2]) for result in results[:4]) + (
        results[4].reshape(-1),
    )


def shards(
    tokens, seq_ids, grad_output, qkv_weight, out_weight, up_weight, down_weight, small_params
):
    weights = gather_all(
        (
            qkv_weight.reshape(-1, 3 * D),
            out_weight.reshape(-1, D),
            up_weight.reshape(-1, FF),
            down_weight.reshape(-1, D),
            small_params.reshape(1, -1),
        )
    )
    result, kept = forward_pass(tokens, seq_ids, weights)
    first_grad, up_grad, down_grad, mlp_small = mlp_backward(grad_output, kept, weights)
    tokens_grad, qkv_grad, out_grad, attn_small = attention_backward(
        tokens, first_grad, kept, weights
    )
    small_grad = jnp.concatenate(list(attn_small) + list(mlp_small))
    down_share, up_share, qkv_share, out_share, small_share = scatter_all(
        [row_blocks(grad.astype(jnp.bfloat16)) for grad in (down_grad, up_grad, qkv_grad, out_grad)]
        + [small_grad.reshape(lax.axis_size("fsdp"), 1, -1)]
    )
    return (
        result,
        tokens_grad,
        qkv_share.reshape(-1),
        out_share.reshape(-1),
        up_share.reshape(-1),
        down_share.reshape(-1),
        small_share.reshape(-1),
    )


def solution(mesh):
    in_specs = (
        P("fsdp", None),
        P("fsdp"),
        P("fsdp", None),
        P("fsdp"),
        P("fsdp"),
        P("fsdp"),
        P("fsdp"),
        P("fsdp"),
    )
    out_specs = (
        P("fsdp", None),
        P("fsdp", None),
        P("fsdp"),
        P("fsdp"),
        P("fsdp"),
        P("fsdp"),
        P("fsdp"),
    )
    return jax.shard_map(shards, mesh=mesh, in_specs=in_specs, out_specs=out_specs, check_vma=False)
```

```python
import functools

import jax
import jax.numpy as jnp
from jax import lax
from jax.experimental import pallas as pl
from jax.experimental.pallas import tpu as pltpu
from jax.sharding import PartitionSpec as P

D = 1024
HEAD_DIM = 64
FF = 4096
TOK_DEV = 128


EPS = 1e-06
ROOT_HALF = 0.7071067811865476
INV_ROOT_TAU = 0.3989422804014327


def matmul(former, latter):
    return jnp.dot(former, latter, preferred_element_type=jnp.float32)


def matmul_tn(former, latter):
    return lax.dot_general(
        former, latter, (((0,), (0,)), ((), ())), preferred_element_type=jnp.float32
    )


def matmul_nt(former, latter):
    return lax.dot_general(
        former, latter, (((1,), (1,)), ((), ())), preferred_element_type=jnp.float32
    )


def unpack(params):
    params = params.astype(jnp.float32)
    bounds = [0, D, 2 * D, 3 * D, 4 * D, 5 * D, 5 * D + FF, 6 * D + FF, 7 * D + FF, 8 * D + FF]
    return [params[bounds[position] : bounds[position + 1]] for position in range(9)]


def norm_forward(values, gain, shift):
    center = values - jnp.mean(values, axis=-1, keepdims=True)
    inverse = lax.rsqrt(jnp.mean(center * center, axis=-1, keepdims=True) + EPS)
    normed = center * inverse
    return (normed * gain + shift, normed, inverse)


def norm_backward(upstream, normed, inverse, gain):
    scaled = upstream * gain
    return inverse * (
        scaled
        - jnp.mean(scaled, axis=-1, keepdims=True)
        - normed * jnp.mean(scaled * normed, axis=-1, keepdims=True)
    )


def gelu_curve(values):
    return 0.5 * values * (1.0 + lax.erf(values * ROOT_HALF))


def gelu_slope(values):
    return (
        0.5 * (1.0 + lax.erf(values * ROOT_HALF))
        + values * jnp.exp(-0.5 * values * values) * INV_ROOT_TAU
    )


def split_heads(matrix):
    return matrix.reshape(-1, TOK_DEV, matrix.shape[1] // HEAD_DIM, HEAD_DIM)


def block_mask(ids):
    blocks = ids.reshape(-1, TOK_DEV)
    return (blocks[:, :, None] == blocks[:, None, :])[:, None]


def masked_scores(queries, key_rows, same_seq):
    scores = jnp.einsum(
        "bqhd,bkhd->bhqk",
        split_heads(queries),
        split_heads(key_rows),
        preferred_element_type=jnp.float32,
    ) * HEAD_DIM ** (-0.5)
    return jnp.where(same_seq, scores, -jnp.inf)


def attend(queries, key_rows, value_rows, same_seq):
    scores = masked_scores(queries, key_rows, same_seq)
    row_max = jnp.max(scores, axis=-1, keepdims=True)
    log_total = row_max + jnp.log(jnp.sum(jnp.exp(scores - row_max), axis=-1, keepdims=True))
    attn_probs = jnp.exp(scores - log_total).astype(jnp.bfloat16)
    context = (
        jnp.einsum(
            "bhqk,bkhd->bqhd",
            attn_probs,
            split_heads(value_rows),
            preferred_element_type=jnp.float32,
        )
        .reshape(-1, queries.shape[1])
        .astype(jnp.bfloat16)
    )
    return (context, log_total)


def attend_back(queries, key_rows, value_rows, same_seq, log_total, context_grad):
    columns = queries.shape[1]
    probs_full = jnp.exp(masked_scores(queries, key_rows, same_seq) - log_total)
    probs_bf = probs_full.astype(jnp.bfloat16)
    prob_grad = jnp.einsum(
        "bqhd,bkhd->bhqk",
        split_heads(context_grad),
        split_heads(value_rows),
        preferred_element_type=jnp.float32,
    )
    value_grad = jnp.einsum(
        "bhqk,bqhd->bkhd", probs_bf, split_heads(context_grad), preferred_element_type=jnp.float32
    ).reshape(-1, columns)
    row_delta = jnp.sum(probs_full * prob_grad, axis=-1, keepdims=True)
    score_grad = (probs_full * (prob_grad - row_delta) * HEAD_DIM ** (-0.5)).astype(jnp.bfloat16)
    query_grad = jnp.einsum(
        "bhqk,bkhd->bqhd", score_grad, split_heads(key_rows), preferred_element_type=jnp.float32
    ).reshape(-1, columns)
    key_grad = jnp.einsum(
        "bhqk,bqhd->bkhd", score_grad, split_heads(queries), preferred_element_type=jnp.float32
    ).reshape(-1, columns)
    return (query_grad, key_grad, value_grad)


def forward_pass(tokens, seq_ids, weights):
    qkv_matrix, out_matrix, up_matrix, down_matrix, bias_gain = weights
    (
        query_bias,
        value_bias,
        out_bias,
        gain_one,
        shift_one,
        up_bias,
        down_bias,
        gain_two,
        shift_two,
    ) = unpack(bias_gain)
    same_seq = block_mask(seq_ids)
    projected = matmul(tokens, qkv_matrix)
    queries = (projected[:, :D] + query_bias).astype(jnp.bfloat16)
    key_rows = projected[:, D : 2 * D].astype(jnp.bfloat16)
    value_rows = (projected[:, 2 * D :] + value_bias).astype(jnp.bfloat16)
    context, log_total = attend(queries, key_rows, value_rows, same_seq)
    first_sum = tokens.astype(jnp.float32) + matmul(context, out_matrix) + out_bias
    first_norm, first_unit, first_inv = norm_forward(first_sum, gain_one, shift_one)
    first_bf = first_norm.astype(jnp.bfloat16)
    hidden_pre = matmul(first_bf, up_matrix) + up_bias
    activated = gelu_curve(hidden_pre).astype(jnp.bfloat16)
    second_sum = first_norm + matmul(activated, down_matrix) + down_bias
    result, second_unit, second_inv = norm_forward(second_sum, gain_two, shift_two)
    kept = (
        same_seq,
        queries,
        key_rows,
        value_rows,
        log_total,
        context,
        first_unit,
        first_inv,
        first_bf,
        hidden_pre,
        activated,
        second_unit,
        second_inv,
    )
    return (result.astype(jnp.bfloat16), kept)


def mlp_backward(grad_output, kept, weights):
    qkv_matrix, out_matrix, up_matrix, down_matrix, bias_gain = weights
    gain_two = unpack(bias_gain)[7]
    first_bf, hidden_pre, activated, second_unit, second_inv = (
        kept[8],
        kept[9],
        kept[10],
        kept[11],
        kept[12],
    )
    out_cot = grad_output.astype(jnp.float32)
    gain_two_grad = jnp.sum(out_cot * second_unit, axis=0)
    shift_two_grad = jnp.sum(out_cot, axis=0)
    second_grad = norm_backward(out_cot, second_unit, second_inv, gain_two)
    down_bias_grad = jnp.sum(second_grad, axis=0)
    second_bf = second_grad.astype(jnp.bfloat16)
    down_grad = matmul_tn(activated, second_bf)
    hidden_grad = matmul_nt(second_bf, down_matrix) * gelu_slope(hidden_pre)
    up_bias_grad = jnp.sum(hidden_grad, axis=0)
    hidden_bf = hidden_grad.astype(jnp.bfloat16)
    up_grad = matmul_tn(first_bf, hidden_bf)
    first_grad = second_grad + matmul_nt(hidden_bf, up_matrix)
    return (
        first_grad,
        up_grad,
        down_grad,
        (up_bias_grad, down_bias_grad, gain_two_grad, shift_two_grad),
    )


def attention_backward(tokens, first_grad, kept, weights):
    qkv_matrix, out_matrix, up_matrix, down_matrix, bias_gain = weights
    gain_one = unpack(bias_gain)[3]
    same_seq, queries, key_rows, value_rows, log_total, context, first_unit, first_inv = kept[:8]
    gain_one_grad = jnp.sum(first_grad * first_unit, axis=0)
    shift_one_grad = jnp.sum(first_grad, axis=0)
    residual_grad = norm_backward(first_grad, first_unit, first_inv, gain_one)
    out_bias_grad = jnp.sum(residual_grad, axis=0)
    residual_bf = residual_grad.astype(jnp.bfloat16)
    out_grad = matmul_tn(context, residual_bf)
    context_grad = matmul_nt(residual_bf, out_matrix).astype(jnp.bfloat16)
    query_grad, key_grad, value_grad = attend_back(
        queries, key_rows, value_rows, same_seq, log_total, context_grad
    )
    query_bias_grad = jnp.sum(query_grad, axis=0)
    value_bias_grad = jnp.sum(value_grad, axis=0)
    joined_bf = jnp.concatenate([query_grad, key_grad, value_grad], axis=1).astype(jnp.bfloat16)
    qkv_grad = matmul_tn(tokens, joined_bf)
    tokens_grad = (residual_grad + matmul_nt(joined_bf, qkv_matrix)).astype(jnp.bfloat16)
    return (
        tokens_grad,
        qkv_grad,
        out_grad,
        (query_bias_grad, value_bias_grad, out_bias_grad, gain_one_grad, shift_one_grad),
    )


def bit_orders(count):
    bits = count.bit_length() - 1
    first = list(range(bits))
    second, third, fourth = list(first), list(first), list(first)
    if bits > 2:
        second[1], second[2] = 2, 1
    if bits > 3:
        third[1:4] = [3, 1, 2]
        fourth[1:4] = [3, 2, 1]
    return first, second, third, fourth


def column_pieces(widths, parts, orders):
    first, second, third, fourth = orders
    cycle = (first, second, third, first, second, fourth)
    plans = []
    for array, (width, count) in enumerate(zip(widths, parts)):
        size = width // count
        for part in range(count):
            plans.append((array, part * size, size, cycle[len(plans) % len(cycle)]))
    return tuple(plans)


def wavefront(pieces, steps):
    pairs = [(piece, step) for piece in range(pieces) for step in range(steps)]
    return sorted(pairs, key=lambda pair: (pair[0] + 3 * pair[1], -pair[1]))


def row_blocks(matrix):
    count = lax.axis_size("fsdp")
    rows, columns = matrix.shape[0] // count, matrix.shape[1]
    folds = max(1, 16 // rows)
    return matrix.reshape(count, rows * folds, columns // folds)


def scatter_kernel(count, plans, arrays, *refs):
    bits = count.bit_length() - 1
    ins, outs = refs[:arrays], refs[arrays : 2 * arrays]
    held = refs[2 * arrays : 2 * arrays + arrays * bits]
    send_sem, recv_sem = refs[2 * arrays + arrays * bits :]
    me = lax.axis_index("fsdp")

    def side(bit):
        return (me // 2**bit) % 2

    def partner(bit):
        return me + 2**bit * (1 - 2 * side(bit))

    barrier = pltpu.get_barrier_semaphore()
    for bit in range(bits):
        pl.semaphore_signal(
            barrier, inc=1, device_id=(partner(bit),), device_id_type=pl.DeviceIdType.MESH
        )
    pl.semaphore_wait(barrier, bits)

    def remote(piece, step, source, target):
        return pltpu.make_async_remote_copy(
            src_ref=source,
            dst_ref=target,
            send_sem=send_sem.at[piece, step],
            recv_sem=recv_sem.at[piece, step],
            device_id=(partner(plans[piece][3][step]),),
            device_id_type=pl.DeviceIdType.MESH,
        )

    def whole(piece, step):
        array, start, size, _ = plans[piece]
        block = held[array * bits + step].at[:, :, pl.ds(start, size)]
        return remote(piece, step, block, block)

    def spot(piece, step, turn, half):
        order = plans[piece][3]
        if step > 0:
            return 2 * turn + half
        row = half * 2 ** order[0]
        for position, bit in enumerate(order[1:]):
            row = row + ((turn // 2**position) % 2) * 2**bit
        return row

    def source_of(piece, step):
        array = plans[piece][0]
        return ins[array] if step == 0 else held[array * bits + step - 1]

    def begin(piece, step):
        array, start, size, order = plans[piece]
        columns = pl.ds(start, size)
        other = 1 - side(order[step])

        def send(turn, carry):
            remote(
                piece,
                step,
                source_of(piece, step).at[spot(piece, step, turn, other), :, columns],
                held[array * bits + step].at[turn, :, columns],
            ).start()
            return carry

        lax.fori_loop(0, count // 2 ** (step + 1), send, 0)

    def add(piece, step):
        array, start, size, order = plans[piece]
        columns = pl.ds(start, size)
        mine = side(order[step])
        target = held[array * bits + step]

        def one(turn, carry):
            kept = source_of(piece, step)[spot(piece, step, turn, mine), :, columns]
            total = kept.astype(jnp.float32) + target[turn, :, columns].astype(jnp.float32)
            if step == bits - 1:
                outs[array][:, columns] = total
            else:
                target[turn, :, columns] = total.astype(target.dtype)
            return carry

        lax.fori_loop(0, count // 2 ** (step + 1), one, 0)

    for piece in range(len(plans)):
        begin(piece, 0)
    for piece, step in wavefront(len(plans), bits):
        whole(piece, step).wait_recv()
        add(piece, step)
        if step + 1 < bits:
            begin(piece, step + 1)
    for piece in range(len(plans)):
        for step in range(bits):
            whole(piece, step).wait_send()


def scatter_all(blocks):
    count = lax.axis_size("fsdp")
    bits = count.bit_length() - 1
    plans = column_pieces(
        [block.shape[2] for block in blocks], (8, 8, 6, 2, 1), bit_orders(count)
    )
    return pl.pallas_call(
        functools.partial(scatter_kernel, count, plans, len(blocks)),
        out_shape=[jax.ShapeDtypeStruct(block.shape[1:], jnp.float32) for block in blocks],
        in_specs=[pl.BlockSpec(memory_space=pltpu.VMEM)] * len(blocks),
        out_specs=[pl.BlockSpec(memory_space=pltpu.VMEM)] * len(blocks),
        scratch_shapes=[
            pltpu.VMEM((count // 2 ** (step + 1),) + block.shape[1:], block.dtype)
            for block in blocks
            for step in range(bits)
        ]
        + [
            pltpu.SemaphoreType.DMA((len(plans), bits)),
            pltpu.SemaphoreType.DMA((len(plans), bits)),
        ],
        compiler_params=pltpu.CompilerParams(
            collective_id=1, has_side_effects=True, vmem_limit_bytes=64000000
        ),
    )(*blocks)


def gather_kernel(count, plans, arrays, *refs):
    ins, outs = refs[:arrays], refs[arrays : 2 * arrays]
    local_sem, send_sem, recv_sem = refs[2 * arrays :]
    me = lax.axis_index("fsdp")
    bits = count.bit_length() - 1

    def partner(bit):
        return me + 2**bit * (1 - 2 * ((me // 2**bit) % 2))

    barrier = pltpu.get_barrier_semaphore()
    for bit in range(bits):
        pl.semaphore_signal(
            barrier, inc=1, device_id=(partner(bit),), device_id_type=pl.DeviceIdType.MESH
        )
    pl.semaphore_wait(barrier, bits)

    def own_copy(piece):
        array, start, size, _ = plans[piece]
        columns = pl.ds(start, size)
        return pltpu.make_async_copy(
            ins[array].at[:, columns], outs[array].at[me, :, columns], local_sem.at[piece]
        )

    def remote(piece, step, source, target):
        return pltpu.make_async_remote_copy(
            src_ref=source,
            dst_ref=target,
            send_sem=send_sem.at[piece, step],
            recv_sem=recv_sem.at[piece, step],
            device_id=(partner(plans[piece][3][step]),),
            device_id_type=pl.DeviceIdType.MESH,
        )

    def whole(piece, step):
        array, start, size, _ = plans[piece]
        block = outs[array].at[pl.ds(0, 2**step), :, pl.ds(start, size)]
        return remote(piece, step, block, block)

    def begin(piece, step):
        array, start, size, order = plans[piece]
        columns = pl.ds(start, size)
        if step == 0:
            remote(
                piece, step, ins[array].at[:, columns], outs[array].at[me, :, columns]
            ).start()
            return
        base = me
        for bit in order[:step]:
            base = base - ((me // 2**bit) % 2) * 2**bit

        def send(turn, carry):
            row = base
            for position, bit in enumerate(order[:step]):
                row = row + ((turn // 2**position) % 2) * 2**bit
            block = outs[array].at[row, :, columns]
            remote(piece, step, block, block).start()
            return carry

        lax.fori_loop(0, 2**step, send, 0)

    pieces = range(len(plans))
    for piece in pieces:
        begin(piece, 0)
    for piece in pieces:
        own_copy(piece).start()
    for piece, step in wavefront(len(plans), bits):
        whole(piece, step).wait_recv()
        if step == 0:
            own_copy(piece).wait()
        if step + 1 < bits:
            begin(piece, step + 1)
    for step in range(bits):
        for piece in pieces:
            whole(piece, step).wait_send()


def gather_all(blocks):
    count = lax.axis_size("fsdp")
    plans = column_pieces(
        [block.shape[1] for block in blocks],
        (6, 2, 8, 8, 1),
        [order[::-1] for order in bit_orders(count)],
    )
    bits = count.bit_length() - 1
    results = pl.pallas_call(
        functools.partial(gather_kernel, count, plans, len(blocks)),
        out_shape=[jax.ShapeDtypeStruct((count,) + block.shape, block.dtype) for block in blocks],
        in_specs=[pl.BlockSpec(memory_space=pltpu.VMEM)] * len(blocks),
        out_specs=[pl.BlockSpec(memory_space=pl.ANY)] * len(blocks),
        scratch_shapes=[
            pltpu.SemaphoreType.DMA((len(plans),)),
            pltpu.SemaphoreType.DMA((len(plans), bits)),
            pltpu.SemaphoreType.DMA((len(plans), bits)),
        ],
        compiler_params=pltpu.CompilerParams(collective_id=0, has_side_effects=True),
    )(*blocks)
    return tuple(result.reshape(-1, result.shape[2]) for result in results[:4]) + (
        results[4].reshape(-1),
    )


def shards(
    tokens, seq_ids, grad_output, qkv_weight, out_weight, up_weight, down_weight, small_params
):
    weights = gather_all(
        (
            qkv_weight.reshape(-1, 3 * D),
            out_weight.reshape(-1, D),
            up_weight.reshape(-1, FF),
            down_weight.reshape(-1, D),
            small_params.reshape(1, -1),
        )
    )
    result, kept = forward_pass(tokens, seq_ids, weights)
    first_grad, up_grad, down_grad, mlp_small = mlp_backward(grad_output, kept, weights)
    tokens_grad, qkv_grad, out_grad, attn_small = attention_backward(
        tokens, first_grad, kept, weights
    )
    small_grad = jnp.concatenate(list(attn_small) + list(mlp_small))
    down_share, up_share, qkv_share, out_share, small_share = scatter_all(
        [row_blocks(grad.astype(jnp.bfloat16)) for grad in (down_grad, up_grad, qkv_grad, out_grad)]
        + [small_grad.reshape(lax.axis_size("fsdp"), 1, -1)]
    )
    return (
        result,
        tokens_grad,
        qkv_share.reshape(-1),
        out_share.reshape(-1),
        up_share.reshape(-1),
        down_share.reshape(-1),
        small_share.reshape(-1),
    )


def solution(mesh):
    in_specs = (
        P("fsdp", None),
        P("fsdp"),
        P("fsdp", None),
        P("fsdp"),
        P("fsdp"),
        P("fsdp"),
        P("fsdp"),
        P("fsdp"),
    )
    out_specs = (
        P("fsdp", None),
        P("fsdp", None),
        P("fsdp"),
        P("fsdp"),
        P("fsdp"),
        P("fsdp"),
        P("fsdp"),
    )
    return jax.shard_map(shards, mesh=mesh, in_specs=in_specs, out_specs=out_specs, check_vma=False)
```
